32 devices in a mesh: dp: 8 (over y, x, core), code: 4 (over z).
Axes of the slice: x: 2, y: 2, z: 4, core: 2. Of those that a mesh axis runs over, the one named last changes fastest.
Arguments:
- temporal_out: bfloat16 [1024, 4096], P('dp'), may hold values from -6 to 6
- depth_in: bfloat16 [4, 4096, 1024], P('code', 'dp'), may hold values from -0.09375 to 0.09375
- embed: bfloat16 [4, 1024, 1024], P('code'), may hold values from -6 to 6
- depth_w1: bfloat16 [4, 1024, 2112], P('code', None, 'dp'), may hold values from -0.1875 to 0.1875
- depth_w2: bfloat16 [4, 1024, 2112], P('code', None, 'dp'), may hold values from -0.125 to 0.125
- audio_tokens: int32 [1024, 4], P(None, 'code'), may hold values from 0 to 1023
- barge_mask: int32 [1024], P('dp'), may hold values 0 or 1
- out_grad: bfloat16 [1024, 4, 1024], P('dp', 'code'), may hold values from -6 to 6
Outputs:
- temporal_grad: bfloat16 [1024, 4096], P('dp', 'code')
- depth_in_grad: bfloat16 [4, 4096, 1024], P('code', 'dp')
- embed_grad: bfloat16 [4, 1024, 1024], P('code', 'dp')
- w1_grad: bfloat16 [4, 1024, 2112], P('code', None, 'dp')
- w2_grad: bfloat16 [4, 1024, 2112], P('code', None, 'dp')
The draws below stay inside these ranges and needn't reach their ends.
All inputs are finite; a program needn't handle non-finite values. No bound on the sum of `barge_mask` on one device may be relied on, other than what follows from the above.
Results may differ from the reference program's by a relative error of at most 0.02.
Values may be sent and summed in bfloat16 or wider, within the bound.
A program may use at most 128 MiB of HBM per device.

```python
import jax
import jax.numpy as jnp
from jax import lax

D = 4096
DD = 1024
DH = 2112
V = 1024
ROWS_DEV = 128
FRAMES = 1024
CODEBOOKS = 4
N_DP = 8


def plant(entries, key, least, high):
    place = [jax.random.randint(jax.random.fold_in(key, axis), (), 0, length) for axis, length in enumerate(entries.shape)]
    main_axis = entries.shape.index(max(entries.shape))
    next_to = place[:main_axis] + [(place[main_axis] + 1) % entries.shape[main_axis]] + place[main_axis + 1:]
    return entries.at[tuple(place)].set(least).at[tuple(next_to)].set(high)


def levels(key, shape, cuts, low, top_value):
    def one(position, parts):
        heights = jax.random.uniform(jax.random.fold_in(jax.random.fold_in(key, 6), position), (parts,), jnp.float32, low / len(cuts), top_value / len(cuts))
        return jnp.repeat(jnp.exp(heights), shape[position] // parts).reshape((-1,) + (1,) * (len(shape) - position - 1))

    gain = one(*cuts[0])
    for cut in cuts[1:]:
        gain = gain * one(*cut)
    return gain


def noise(key, extent, deviation, bound, pieces=(), held_as=jnp.bfloat16):
    level = levels(key, extent, pieces, -0.22, 0.18) if pieces else 1.0
    values = jax.random.normal(key, extent, jnp.float32) * deviation * level
    return jnp.minimum(jnp.maximum(values, -bound), bound).astype(held_as)


def setup_inputs(seed: int = 0) -> dict:
    streams_of = jax.random.split(jax.random.key(seed), 9)
    return {
        "temporal_out": noise(streams_of[0], (FRAMES, D), 1.0, 6.0, ((0, 8),)),
        "depth_in": noise(streams_of[1], (CODEBOOKS, D, DD), D ** -0.5, 0.09375, ((0, 4), (1, 8))),
        "embed": noise(streams_of[2], (CODEBOOKS, V, DD), 1.0, 6.0, ((0, 4),)),
        "depth_w1": noise(streams_of[3], (CODEBOOKS, DD, DH), DD ** -0.5, 0.1875, ((0, 4), (2, 8))),
        "depth_w2": noise(streams_of[4], (CODEBOOKS, DD, DH), DH ** -0.5, 0.125, ((0, 4), (2, 8))),
        "audio_tokens": plant(jax.random.randint(streams_of[5], (FRAMES, CODEBOOKS), 0, V), jax.random.fold_in(streams_of[5], 1), 0, V - 1).astype(jnp.int32),
        "barge_mask": plant((jax.random.randint(streams_of[6], (FRAMES,), 0, 2) < 1).astype(jnp.int32), jax.random.fold_in(streams_of[6], 1), 0, 1),
        "out_grad": noise(streams_of[7], (FRAMES, CODEBOOKS, DD), 1.0, 6.0, ((0, 8), (1, 4))),
    }


EPS = 1e-06

def matmul(left, right):
    return jnp.dot(left, right, preferred_element_type=jnp.float32)

def contract_rows(left, right):
    return lax.dot_general(left, right, (((0,), (0,)), ((), ())), preferred_element_type=jnp.float32)

def contract_cols(left, right):
    return lax.dot_general(left, right, (((1,), (1,)), ((), ())), preferred_element_type=jnp.float32)

def silu_slope(values):
    sigma = jax.nn.sigmoid(values)
    return sigma * (1.0 + values * (1.0 - sigma))

def group_sum(left, right):
    total = jnp.zeros((left.shape[1], right.shape[1]), jnp.float32)
    for group in range(N_DP):
        first = group * ROWS_DEV
        part = contract_rows(left[first:first + ROWS_DEV], right[first:first + ROWS_DEV]).astype(jnp.bfloat16)
        total = total + part.astype(jnp.float32)
    return total.astype(jnp.bfloat16)

def reference(temporal_out, depth_in, embed, depth_w1, depth_w2, audio_tokens, barge_mask, out_grad):
    row_weight = barge_mask.astype(jnp.float32)[:, None]
    incoming = jnp.zeros((FRAMES, DD), jnp.bfloat16)
    saved = []
    for book in range(CODEBOOKS):
        table_rows = jnp.take(embed[book], audio_tokens[:, book], axis=0).astype(jnp.float32)
        resid = matmul(temporal_out, depth_in[book]) + table_rows + incoming.astype(jnp.float32)
        scale = lax.rsqrt(lax.optimization_barrier(jnp.mean(resid * resid, axis=-1, keepdims=True)) + EPS)
        normed = (resid * scale).astype(jnp.bfloat16)
        pre_act = matmul(normed, depth_w1[book])
        active = jax.nn.silu(pre_act).astype(jnp.bfloat16)
        incoming = (resid + contract_cols(active, depth_w2[book])).astype(jnp.bfloat16)
        saved.append((resid, scale, normed, pre_act, active))
    vocab_ids = jnp.arange(V, dtype=jnp.int32)[None, :]
    from_next = jnp.zeros((FRAMES, DD), jnp.bfloat16)
    temporal_slope = jnp.zeros((FRAMES, D), jnp.float32)
    w1_list = [None] * CODEBOOKS
    w2_list = [None] * CODEBOOKS
    in_list = [None] * CODEBOOKS
    embed_list = [None] * CODEBOOKS
    for book in reversed(range(CODEBOOKS)):
        resid, scale, normed, pre_act, active = saved[book]
        state_slope = out_grad[:, book, :].astype(jnp.float32) * row_weight + from_next.astype(jnp.float32)
        slope_b = state_slope.astype(jnp.bfloat16)
        pre_slope = (matmul(slope_b, depth_w2[book]) * silu_slope(pre_act)).astype(jnp.bfloat16)
        norm_slope = contract_cols(pre_slope, depth_w1[book])
        unit_rows = resid * scale
        from_next = (state_slope + scale * (norm_slope - unit_rows * lax.optimization_barrier(jnp.mean(norm_slope * unit_rows, axis=-1, keepdims=True)))).astype(jnp.bfloat16)
        w1_list[book] = group_sum(normed, pre_slope)
        w2_list[book] = group_sum(slope_b, active)
        in_list[book] = group_sum(temporal_out, from_next)
        onehot = (audio_tokens[:, book][:, None] == vocab_ids).astype(jnp.bfloat16)
        embed_list[book] = group_sum(onehot, from_next)
        term = contract_cols(from_next, depth_in[book]).astype(jnp.bfloat16)
        temporal_slope = temporal_slope + term.astype(jnp.float32)
    temporal_grad = temporal_slope.astype(jnp.bfloat16)
    return (temporal_grad, jnp.stack(in_list), jnp.stack(embed_list), jnp.stack(w1_list), jnp.stack(w2_list))
```

```python
import functools

import jax
import jax.numpy as jnp
from jax import lax
from jax.experimental import pallas as pl
from jax.experimental.pallas import tpu as pltpu
from jax.sharding import PartitionSpec as P

EPS = 1e-06
MESH = pl.DeviceIdType.MESH
CHUNKS = 4
BF16, F32 = jnp.bfloat16, jnp.float32


def dot_nn(left, right):
    return jnp.dot(left, right, preferred_element_type=F32)


def dot_tn(left, right):
    return lax.dot_general(left, right, (((0,), (0,)), ((), ())), preferred_element_type=F32)


def chain_kernel(
    n_dp,
    n_code,
    temporal_hbm,
    cot_hbm,
    table_hbm,
    token_hbm,
    mask_hbm,
    proj_own,
    w1_own,
    w2_own,
    temporal_grad,
    proj_grad,
    table_grad,
    w1_grad,
    w2_grad,
    temporal,
    cot_ref,
    token,
    mask,
    proj,
    w1,
    w2,
    proj_t,
    w1_t,
    w2_t,
    base,
    incoming,
    returning,
    state,
    pre_ref,
    act,
    slope_h,
    act_t,
    pre_t,
    scale_ref,
    term,
    term_in,
    cols_all,
    normed_all,
    slope_all,
    carry_all,
    act_all,
    pre_all,
    load_sem,
    ring_send,
    ring_recv,
    pass_send,
    pass_recv,
    own_sem,
    chain_send,
    chain_recv,
    ag_send,
    ag_recv,
    swap_send,
    swap_recv,
    term_send,
    term_recv,
):
    dp = lax.axis_index("dp")
    code = lax.axis_index("code")
    rows, width = base.shape
    hidden = w1.shape[0]
    pad = hidden // n_dp
    share = w1_grad.shape[0]
    used = w1_own.shape[0]
    depth = proj_own.shape[0]
    half = width // 2
    step_rows = rows // CHUNKS
    chips = n_dp // 2
    core = lax.rem(dp, 2)
    chip = dp // 2
    partner = chip * 2 + 1 - core
    first = code == 0
    last = code == n_code - 1

    def ring_place(c):
        return jnp.where(lax.rem(c, 2) == 0, c // 2, chips - 1 - c // 2)

    def ring_chip(p):
        p = lax.rem(p + 2 * chips, chips)
        return jnp.where(p < chips // 2, 2 * p, 2 * (chips - 1 - p) + 1)

    place = ring_place(chip)
    right = ring_chip(place + 1) * 2 + core
    left = ring_chip(place - 1) * 2 + core

    loads = [
        pltpu.make_async_copy(src, dst, load_sem.at[i])
        for i, (src, dst) in enumerate(
            (
                (temporal_hbm, temporal),
                (cot_hbm, cot_ref),
                (table_hbm, w2_t.at[pl.ds(0, table_hbm.shape[0]), pl.ds(0, width)]),
                (token_hbm, token),
                (mask_hbm, mask),
            )
        )
    ]

    barrier = pltpu.get_barrier_semaphore()
    for other in range(1, n_dp):
        pl.semaphore_signal(
            barrier, inc=1, device_id=(lax.rem(dp + other, n_dp), code), device_id_type=MESH
        )
    for other in range(1, n_code):
        pl.semaphore_signal(
            barrier, inc=1, device_id=(dp, lax.rem(code + other, n_code)), device_id_type=MESH
        )
    for load in loads:
        load.start()
    if pad > used:
        for owner in range(n_dp):
            fill = jnp.zeros((pad - used, width), BF16)
            w1[owner * pad + used : (owner + 1) * pad, :] = fill
            w2[owner * pad + used : (owner + 1) * pad, :] = fill
    pl.semaphore_wait(barrier, n_dp + n_code - 2)

    whole = (
        (proj_own, proj, depth, depth),
        (w1_own, w1, pad, used),
        (w2_own, w2, pad, used),
    )

    def part(i, owner, way):
        _, full, size, filled = whole[i]
        start = pl.multiple_of(owner * size, 16)
        return full.at[pl.ds(start, filled), pl.ds(way * half, half)]

    def origin_of(way, step):
        return ring_chip(place - step if way == 0 else place + step) * 2 + core

    def ring_copy(i, way, step):
        dst = part(i, origin_of(way, step), way)
        src = whole[i][0].at[:, pl.ds(way * half, half)] if step == 0 else dst
        return pltpu.make_async_remote_copy(
            src_ref=src,
            dst_ref=dst,
            send_sem=ring_send.at[i, way, step],
            recv_sem=ring_recv.at[i, way, step],
            device_id=(right if way == 0 else left, code),
            device_id_type=MESH,
        )

    def pass_copy(i, way, step):
        dst = part(i, origin_of(way, step), way)
        src = whole[i][0].at[:, pl.ds(way * half, half)] if step == 0 else dst
        return pltpu.make_async_remote_copy(
            src_ref=src,
            dst_ref=dst,
            send_sem=pass_send.at[i, way, step],
            recv_sem=pass_recv.at[i, way, step],
            device_id=(partner, code),
            device_id_type=MESH,
        )

    def own_copy(i):
        own, full, size, filled = whole[i]
        start = pl.multiple_of(dp * size, 16)
        return pltpu.make_async_copy(own, full.at[pl.ds(start, filled), :], own_sem.at[i])

    def add_base(origin, way):
        lanes = pl.ds(way * half, half)
        spot = pl.ds(pl.multiple_of(origin * depth, 128), depth)
        block = proj[pl.ds(pl.multiple_of(origin * depth, 16), depth), lanes]
        base[:, lanes] += dot_nn(temporal[:, spot], block)
        proj_t[lanes, spot] = block.T

    def flip(source, target):
        def turn(t, carry):
            spot = pl.ds(pl.multiple_of(t * 128, 128), 128)
            target[:, spot] = source[spot, :].T
            return carry

        lax.fori_loop(0, hidden // 128, turn, 0)
        rest = hidden % 128
        if rest:
            target[:, hidden - rest :] = source[hidden - rest :, :].T

    def swap_copy(i, other):
        target = lax.rem(dp + other, n_dp)
        spot = pl.ds(pl.multiple_of(dp * rows, 128), rows)
        if i == 0:
            src = temporal.at[:, pl.ds(pl.multiple_of(target * depth, 128), depth)]
            dst = cols_all.at[dp]
        else:
            source, full = ((act_t, act_all), (pre_t, pre_all))[i - 1]
            src = source.at[pl.ds(pl.multiple_of(target * pad, 16), pad), :]
            dst = full.at[:, spot]
        return pltpu.make_async_remote_copy(
            src_ref=src,
            dst_ref=dst,
            send_sem=swap_send.at[i, other],
            recv_sem=swap_recv.at[i, other],
            device_id=(target, code),
            device_id_type=MESH,
        )

    gathered = (normed_all, slope_all, carry_all)

    def peer_copy(i, other):
        block = gathered[i].at[dp]
        target = lax.rem(dp + 2 * other, n_dp)
        return pltpu.make_async_remote_copy(
            src_ref=block,
            dst_ref=block,
            send_sem=ag_send.at[i, 0, other],
            recv_sem=ag_recv.at[i, 0, other],
            device_id=(target, code),
            device_id_type=MESH,
        )

    def hand_copy(i, other):
        block = gathered[i].at[lax.rem(dp - 2 * other + n_dp, n_dp)]
        return pltpu.make_async_remote_copy(
            src_ref=block,
            dst_ref=block,
            send_sem=ag_send.at[i, 1, other],
            recv_sem=ag_recv.at[i, 1, other],
            device_id=(partner, code),
            device_id_type=MESH,
        )

    def gather_start(i):
        for other in range(1, chips):
            peer_copy(i, other).start()
        hand_copy(i, 0).start()

    def gather_forward(i):
        for other in range(1, chips):
            peer_copy(i, other).wait_recv()
            hand_copy(i, other).start()

    def gather_finish(i):
        for other in range(1, chips):
            peer_copy(i, other).wait_send()
        for other in range(chips):
            hand_copy(i, other).wait()

    def chain_copy(way, c):
        chunk = pl.ds(pl.multiple_of(c * step_rows, step_rows), step_rows)
        src = state.at[chunk, :] if way == 0 else carry_all.at[dp, chunk, :]
        dst = (incoming, returning)[way]
        target = lax.rem(code + (1 if way == 0 else n_code - 1), n_code)
        return pltpu.make_async_remote_copy(
            src_ref=src,
            dst_ref=dst.at[chunk, :],
            send_sem=chain_send.at[way, c],
            recv_sem=chain_recv.at[way, c],
            device_id=(dp, target),
            device_id_type=MESH,
        )

    def forward_up(chunk, resid):
        size = resid.shape[0]
        base[chunk, :] = resid
        scale = lax.rsqrt(jnp.mean(resid * resid, axis=-1, keepdims=True) + EPS)
        scale_ref[chunk, :] = jnp.broadcast_to(scale, (size, 128))
        normed = (resid * scale).astype(BF16)
        normed_all[dp, chunk, :] = normed
        pre = dot_nn(normed, w1_t[...])
        pre_ref[chunk, :] = pre
        act[chunk, :] = (pre * jax.nn.sigmoid(pre)).astype(BF16)

    def forward_down(chunk):
        state[chunk, :] = (base[chunk, :] + dot_nn(act[chunk, :], w2[...])).astype(BF16)

    def backward(chunk, slope):
        slope_b = slope.astype(BF16)
        slope_all[dp, chunk, :] = slope_b
        back = dot_nn(slope_b, w2_t[...])
        pre = pre_ref[chunk, :]
        sigma = jax.nn.sigmoid(pre)
        slope_h[chunk, :] = (back * (sigma * (1.0 + pre * (1.0 - sigma)))).astype(BF16)
        norm_slope = dot_nn(slope_h[chunk, :], w1[...])
        scale = scale_ref[chunk, 0:1]
        unit = base[chunk, :] * scale
        carry_all[dp, chunk, :] = (
            slope
            + scale * (norm_slope - unit * jnp.mean(norm_slope * unit, axis=-1, keepdims=True))
        ).astype(BF16)

    def over_chunks(body):
        def turn(c, carry):
            body(c, pl.ds(pl.multiple_of(c * step_rows, step_rows), step_rows))
            return carry

        lax.fori_loop(0, CHUNKS, turn, 0)

    every = pl.ds(0, rows)

    for i in range(3):
        for way in range(2):
            ring_copy(i, way, 0).start()
    for i in range(3):
        for way in range(2):
            pass_copy(i, way, 0).start()
        own_copy(i).start()

    for load in loads:
        load.wait()
    own_rows = pl.ds(pl.multiple_of(dp * rows, 128), rows)
    vocab = table_hbm.shape[0]
    picked = lax.broadcasted_iota(jnp.int32, (vocab, rows), 0) == token[:, own_rows]
    base[...] = dot_tn(picked.astype(F32).astype(BF16), w2_t[:vocab, :width])
    line = lax.broadcasted_iota(jnp.int32, (rows, rows), 0)
    spread = lax.broadcasted_iota(jnp.int32, (rows, rows), 1)
    keep = jnp.where(line == spread, mask[...].astype(F32), 0.0).astype(BF16)
    cot_ref[...] = dot_nn(keep, cot_ref[...]).astype(BF16)

    own_copy(0).wait()
    for way in range(2):
        add_base(dp, way)
    for step in range(1, chips):
        for i in range(3):
            for way in range(2):
                ring_copy(i, way, step - 1).wait_recv()
                if step < chips - 1:
                    ring_copy(i, way, step).start()
                pass_copy(i, way, step).start()
            if i == 0:
                for way in range(2):
                    add_base(origin_of(way, step), way)
                for way in range(2):
                    pass_copy(0, way, step - 1).wait_recv()
                    add_base(origin_of(way, step - 1) + 1 - 2 * core, way)
            if i == 1 and step == chips - 1:
                for way in range(2):
                    pass_copy(0, way, chips - 1).wait_recv()
                    add_base(origin_of(way, chips - 1) + 1 - 2 * core, way)
                own_copy(1).wait()
                for way in range(2):
                    for back in range(chips):
                        pass_copy(1, way, back).wait_recv()
                flip(w1, w1_t)

    @pl.when(first)
    def _():
        forward_up(every, base[...])

    own_copy(2).wait()
    for way in range(2):
        for step in range(chips):
            pass_copy(2, way, step).wait_recv()

    @pl.when(first)
    def _():
        forward_down(every)
        for c in range(CHUNKS):
            chain_copy(0, c).start()

    for other in range(1, n_dp):
        swap_copy(0, other).start()
    cols_all[dp] = temporal[:, pl.ds(pl.multiple_of(dp * depth, 128), depth)]
    flip(w2, w2_t)

    @pl.when(jnp.logical_not(first))
    def _():
        def body(c, chunk):
            chain_copy(0, c).wait_recv()
            forward_up(chunk, base[chunk, :] + incoming[chunk, :].astype(F32))
            forward_down(chunk)

            @pl.when(jnp.logical_not(last))
            def _():
                chain_copy(0, c).start()

        over_chunks(body)

    gather_start(0)

    def send_act():
        act_t[...] = act[...].T
        for other in range(1, n_dp):
            swap_copy(1, other).start()
        act_all[:, own_rows] = act_t[pl.ds(pl.multiple_of(dp * pad, 16), pad), :]

    @pl.when(last)
    def _():
        backward(every, cot_ref[...].astype(F32))
        for c in range(CHUNKS):
            chain_copy(1, c).start()

    send_act()

    @pl.when(first)
    def _():
        gather_forward(0)

    @pl.when(jnp.logical_not(last))
    def _():
        def body(c, chunk):
            chain_copy(1, c).wait_recv()
            slope = cot_ref[chunk, :].astype(F32) + returning[chunk, :].astype(F32)
            backward(chunk, slope)

            @pl.when(jnp.logical_not(first))
            def _():
                chain_copy(1, c).start()

        over_chunks(body)

    gather_start(1)
    gather_start(2)

    @pl.when(jnp.logical_not(first))
    def _():
        gather_forward(0)

    quarter = term.shape[2]
    early = code * 2 < n_code

    def term_copy(other):
        target = lax.rem(code + other, n_code)
        return pltpu.make_async_remote_copy(
            src_ref=term.at[target],
            dst_ref=term_in.at[other],
            send_sem=term_send.at[other],
            recv_sem=term_recv.at[other],
            device_id=(dp, target),
            device_id_type=MESH,
        )

    for other in reversed(range(n_code)):
        target = lax.rem(code + other, n_code)
        spot = pl.ds(pl.multiple_of(target * quarter, 128), quarter)
        term[target] = dot_nn(carry_all[dp], proj_t[:, spot]).astype(BF16)
        if other:

            @pl.when(early)
            def _():
                term_copy(other).start()

    pre_t[...] = slope_h[...].T
    for other in range(1, n_dp):
        swap_copy(2, other).start()
    pre_all[:, own_rows] = pre_t[pl.ds(pl.multiple_of(dp * pad, 16), pad), :]

    gather_forward(1)
    gather_forward(2)

    @pl.when(jnp.logical_not(early))
    def _():
        for other in range(1, n_code):
            term_copy(other).start()

    def all_rows(array):
        return array[...].reshape(n_dp * rows, array.shape[2])

    gather_finish(0)
    gather_finish(1)
    for other in range(1, n_dp):
        swap_copy(1, other).wait()
    w2_grad[...] = dot_nn(act_all[...], all_rows(slope_all)).astype(BF16)[:share]
    for other in range(1, n_dp):
        swap_copy(2, other).wait()
    w1_grad[...] = dot_nn(pre_all[...], all_rows(normed_all)).astype(BF16)[:share]
    gather_finish(2)
    for other in range(1, n_dp):
        swap_copy(0, other).wait()
    carries = all_rows(carry_all)
    proj_grad[...] = dot_tn(all_rows(cols_all), carries).astype(BF16)
    piece = table_grad.shape[0]
    ids = lax.broadcasted_iota(jnp.int32, (piece, n_dp * rows), 0) + dp * piece
    table_grad[...] = dot_nn((ids == token[...]).astype(F32).astype(BF16), carries).astype(BF16)

    total = term[code].astype(F32)
    for other in range(1, n_code):
        term_copy(other).wait_recv()
        total += term_in[other].astype(F32)
    temporal_grad[...] = total.astype(BF16)

    for i in range(3):
        for way in range(2):
            for step in range(chips - 1):
                ring_copy(i, way, step).wait_send()
            for step in range(chips):
                pass_copy(i, way, step).wait_send()
    for c in range(CHUNKS):

        @pl.when(jnp.logical_not(last))
        def _():
            chain_copy(0, c).wait_send()

        @pl.when(jnp.logical_not(first))
        def _():
            chain_copy(1, c).wait_send()

    for other in range(1, n_code):
        term_copy(other).wait_send()


def per_device(
    temporal_out, depth_in, embed, depth_w1, depth_w2, audio_tokens, barge_mask, out_grad
):
    n_code = lax.axis_size("code")
    n_dp = lax.axis_size("dp")
    rows, wide = temporal_out.shape
    depth, width = depth_in.shape[1:]
    share = depth_w1.shape[2]
    pad = -(-share // 16) * 16
    hidden = pad * n_dp
    quarter = wide // n_code
    chips = n_dp // 2
    vocab = embed.shape[1]
    frames = audio_tokens.shape[0]
    extra = ((0, -share % 8), (0, 0))

    vmem = pl.BlockSpec(memory_space=pltpu.VMEM)
    hbm = pl.BlockSpec(memory_space=pl.ANY)
    dma = pltpu.SemaphoreType.DMA
    out_shape = (
        jax.ShapeDtypeStruct((rows, quarter), BF16),
        jax.ShapeDtypeStruct((depth, width), BF16),
        jax.ShapeDtypeStruct((vocab // n_dp, width), BF16),
        jax.ShapeDtypeStruct((share, width), BF16),
        jax.ShapeDtypeStruct((share, width), BF16),
    )
    temporal_grad, proj_grad, table_grad, w1_grad, w2_grad = pl.pallas_call(
        functools.partial(chain_kernel, n_dp, n_code),
        out_shape=out_shape,
        in_specs=[hbm] * 8,
        out_specs=(vmem,) * 5,
        scratch_shapes=[
            pltpu.VMEM((rows, wide), BF16),
            pltpu.VMEM((rows, width), BF16),
            pltpu.VMEM((1, frames), jnp.int32),
            pltpu.VMEM((1, rows), jnp.int32),
            pltpu.VMEM((wide, width), BF16),
            pltpu.VMEM((hidden, width), BF16),
            pltpu.VMEM((hidden, width), BF16),
            pltpu.VMEM((width, wide), BF16),
            pltpu.VMEM((width, hidden), BF16),
            pltpu.VMEM((width, hidden), BF16),
            pltpu.VMEM((rows, width), F32),
            pltpu.VMEM((rows, width), BF16),
            pltpu.VMEM((rows, width), BF16),
            pltpu.VMEM((rows, width), BF16),
            pltpu.VMEM((rows, hidden), F32),
            pltpu.VMEM((rows, hidden), BF16),
            pltpu.VMEM((rows, hidden), BF16),
            pltpu.VMEM((hidden, rows), BF16),
            pltpu.VMEM((hidden, rows), BF16),
            pltpu.VMEM((rows, 128), F32),
            pltpu.VMEM((n_code, rows, quarter), BF16),
            pltpu.VMEM((n_code, rows, quarter), BF16),
            pltpu.VMEM((n_dp, rows, depth), BF16),
            pltpu.VMEM((n_dp, rows, width), BF16),
            pltpu.VMEM((n_dp, rows, width), BF16),
            pltpu.VMEM((n_dp, rows, width), BF16),
            pltpu.VMEM((pad, frames), BF16),
            pltpu.VMEM((pad, frames), BF16),
            dma((5,)),
            dma((3, 2, chips)),
            dma((3, 2, chips)),
            dma((3, 2, chips)),
            dma((3, 2, chips)),
            dma((3,)),
            dma((2, CHUNKS)),
            dma((2, CHUNKS)),
            dma((3, 2, chips)),
            dma((3, 2, chips)),
            dma((3, n_dp)),
            dma((3, n_dp)),
            dma((n_code,)),
            dma((n_code,)),
        ],
        compiler_params=pltpu.CompilerParams(
            collective_id=0, has_side_effects=True, vmem_limit_bytes=63 * 1024 * 1024
        ),
        name="depth_chain",
    )(
        temporal_out,
        out_grad[:, 0, :],
        embed[0],
        audio_tokens.reshape(1, frames),
        barge_mask.reshape(1, rows),
        depth_in[0],
        jnp.pad(depth_w1[0].T, extra),
        jnp.pad(depth_w2[0].T, extra),
    )
    return (
        temporal_grad,
        proj_grad[None],
        table_grad[None],
        w1_grad.T[None],
        w2_grad.T[None],
    )


def solution(mesh):
    in_specs = (
        P("dp", None),
        P("code", "dp", None),
        P("code", None, None),
        P("code", None, "dp"),
        P("code", None, "dp"),
        P(None, "code"),
        P("dp"),
        P("dp", "code", None),
    )
    out_specs = (
        P("dp", "code"),
        P("code", "dp", None),
        P("code", "dp", None),
        P("code", None, "dp"),
        P("code", None, "dp"),
    )
    return jax.shard_map(
        per_device, mesh=mesh, in_specs=in_specs, out_specs=out_specs, check_vma=False
    )
```

```python
import functools

import jax
import jax.numpy as jnp
from jax import lax
from jax.experimental import pallas as pl
from jax.experimental.pallas import tpu as pltpu
from jax.sharding import PartitionSpec as P

EPS = 1e-06
MESH = pl.DeviceIdType.MESH
CHUNKS = 4
BF16, F32 = jnp.bfloat16, jnp.float32


def dot_nn(left, right):
    return jnp.dot(left, right, preferred_element_type=F32)


def dot_tn(left, right):
    return lax.dot_general(left, right, (((0,), (0,)), ((), ())), preferred_element_type=F32)


def chain_kernel(
    n_dp,
    n_code,
    temporal_hbm,
    cot_hbm,
    table_hbm,
    token_hbm,
    mask_hbm,
    proj_own,
    w1_own,
    w2_own,
    temporal_out,
    proj_out,
    table_out,
    w1_out,
    w2_out,
    temporal,
    cot_ref,
    token,
    mask,
    proj,
    w1,
    w2,
    proj_t,
    w1_t,
    w2_t,
    base,
    incoming,
    returning,
    state,
    pre_ref,
    act,
    slope_h,
    act_t,
    pre_t,
    scale_ref,
    term,
    term_in,
    cols_all,
    normed_all,
    slope_all,
    carry_all,
    act_all,
    pre_all,
    temporal_grad,
    proj_grad,
    table_grad,
    w1_grad,
    w2_grad,
    load_sem,
    ring_send,
    ring_recv,
    pass_send,
    pass_recv,
    own_sem,
    chain_send,
    chain_recv,
    ag_send,
    ag_recv,
    hand_send,
    hand_recv,
    swap_send,
    swap_recv,
    up_send,
    up_recv,
    down_send,
    down_recv,
    store_sem,
):
    dp = lax.axis_index("dp")
    code = lax.axis_index("code")
    rows, width = base.shape
    hidden = w1.shape[0]
    pad = hidden // n_dp
    share = w1_grad.shape[0]
    used = w1_own.shape[0]
    depth = proj_own.shape[0]
    half = width // 2
    step_rows = rows // CHUNKS
    chips = n_dp // 2
    core = lax.rem(dp, 2)
    chip = dp // 2
    partner = chip * 2 + 1 - core
    first = code == 0
    last = code == n_code - 1

    def ring_place(c):
        return jnp.where(lax.rem(c, 2) == 0, c // 2, chips - 1 - c // 2)

    def ring_chip(p):
        p = lax.rem(p + 2 * chips, chips)
        return jnp.where(p < chips // 2, 2 * p, 2 * (chips - 1 - p) + 1)

    place = ring_place(chip)
    right = ring_chip(place + 1) * 2 + core
    left = ring_chip(place - 1) * 2 + core

    loads = [
        pltpu.make_async_copy(src, dst, load_sem.at[i])
        for i, (src, dst) in enumerate(
            (
                (temporal_hbm, temporal),
                (cot_hbm, cot_ref),
                (table_hbm, w2_t.at[pl.ds(0, table_hbm.shape[0]), pl.ds(0, width)]),
                (token_hbm, token),
                (mask_hbm, mask),
            )
        )
    ]

    barrier = pltpu.get_barrier_semaphore()
    for other in range(1, n_dp):
        pl.semaphore_signal(
            barrier, inc=1, device_id=(lax.rem(dp + other, n_dp), code), device_id_type=MESH
        )
    for other in range(1, n_code):
        pl.semaphore_signal(
            barrier, inc=1, device_id=(dp, lax.rem(code + other, n_code)), device_id_type=MESH
        )
    for load in loads:
        load.start()
    if pad > used:
        for owner in range(n_dp):
            fill = jnp.zeros((pad - used, width), BF16)
            w1[owner * pad + used : (owner + 1) * pad, :] = fill
            w2[owner * pad + used : (owner + 1) * pad, :] = fill
    pl.semaphore_wait(barrier, n_dp + n_code - 2)

    whole = (
        (proj_own, proj, depth, depth),
        (w1_own, w1, pad, used),
        (w2_own, w2, pad, used),
    )

    def part(i, owner, way):
        _, full, size, filled = whole[i]
        start = pl.multiple_of(owner * size, 16)
        return full.at[pl.ds(start, filled), pl.ds(way * half, half)]

    def origin_of(way, step):
        return ring_chip(place - step if way == 0 else place + step) * 2 + core

    def ring_copy(i, way, step):
        dst = part(i, origin_of(way, step), way)
        src = whole[i][0].at[:, pl.ds(way * half, half)] if step == 0 else dst
        return pltpu.make_async_remote_copy(
            src_ref=src,
            dst_ref=dst,
            send_sem=ring_send.at[i, way, step],
            recv_sem=ring_recv.at[i, way, step],
            device_id=(right if way == 0 else left, code),
            device_id_type=MESH,
        )

    def pass_copy(i, way, step):
        dst = part(i, origin_of(way, step), way)
        src = whole[i][0].at[:, pl.ds(way * half, half)] if step == 0 else dst
        return pltpu.make_async_remote_copy(
            src_ref=src,
            dst_ref=dst,
            send_sem=pass_send.at[i, way, step],
            recv_sem=pass_recv.at[i, way, step],
            device_id=(partner, code),
            device_id_type=MESH,
        )

    def own_copy(i):
        own, full, size, filled = whole[i]
        start = pl.multiple_of(dp * size, 16)
        return pltpu.make_async_copy(own, full.at[pl.ds(start, filled), :], own_sem.at[i])

    def add_base(origin, way):
        lanes = pl.ds(way * half, half)
        spot = pl.ds(pl.multiple_of(origin * depth, 128), depth)
        block = proj[pl.ds(pl.multiple_of(origin * depth, 16), depth), lanes]
        base[:, lanes] += dot_nn(temporal[:, spot], block)
        proj_t[lanes, spot] = block.T

    def flip(source, target):
        def turn(t, carry):
            spot = pl.ds(pl.multiple_of(t * 128, 128), 128)
            target[:, spot] = source[spot, :].T
            return carry

        lax.fori_loop(0, hidden // 128, turn, 0)
        rest = hidden % 128
        if rest:
            target[:, hidden - rest :] = source[hidden - rest :, :].T

    def swap_copy(i, other):
        target = lax.rem(dp + other, n_dp)
        spot = pl.ds(pl.multiple_of(dp * rows, 128), rows)
        if i == 0:
            src = temporal.at[:, pl.ds(pl.multiple_of(target * depth, 128), depth)]
            dst = cols_all.at[dp]
        else:
            source, full = ((act_t, act_all), (pre_t, pre_all))[i - 1]
            src = source.at[pl.ds(pl.multiple_of(target * pad, 16), pad), :]
            dst = full.at[:, spot]
        return pltpu.make_async_remote_copy(
            src_ref=src,
            dst_ref=dst,
            send_sem=swap_send.at[i, other],
            recv_sem=swap_recv.at[i, other],
            device_id=(target, code),
            device_id_type=MESH,
        )

    gathered = (normed_all, slope_all, carry_all)

    def peer_copy(i, other, c):
        block = gathered[i].at[dp, pl.ds(pl.multiple_of(c * step_rows, step_rows), step_rows), :]
        target = lax.rem(dp + 2 * other, n_dp)
        return pltpu.make_async_remote_copy(
            src_ref=block,
            dst_ref=block,
            send_sem=ag_send.at[i, other, c],
            recv_sem=ag_recv.at[i, other, c],
            device_id=(target, code),
            device_id_type=MESH,
        )

    def hand_copy(i, other):
        block = gathered[i].at[lax.rem(dp - 2 * other + n_dp, n_dp)]
        return pltpu.make_async_remote_copy(
            src_ref=block,
            dst_ref=block,
            send_sem=hand_send.at[i, other],
            recv_sem=hand_recv.at[i, other],
            device_id=(partner, code),
            device_id_type=MESH,
        )

    def spread(i, c):
        for other in range(1, chips):
            peer_copy(i, other, c).start()

    def gather_forward(i):
        hand_copy(i, 0).start()
        for other in range(1, chips):
            for c in range(CHUNKS):
                peer_copy(i, other, c).wait_recv()
            hand_copy(i, other).start()

    def gather_finish(i):
        for other in range(1, chips):
            for c in range(CHUNKS):
                peer_copy(i, other, c).wait_send()
        for other in range(chips):
            hand_copy(i, other).wait()

    def chain_copy(way, c):
        chunk = pl.ds(pl.multiple_of(c * step_rows, step_rows), step_rows)
        src = state.at[chunk, :] if way == 0 else carry_all.at[dp, chunk, :]
        dst = (incoming, returning)[way]
        target = lax.rem(code + (1 if way == 0 else n_code - 1), n_code)
        return pltpu.make_async_remote_copy(
            src_ref=src,
            dst_ref=dst.at[chunk, :],
            send_sem=chain_send.at[way, c],
            recv_sem=chain_recv.at[way, c],
            device_id=(dp, target),
            device_id_type=MESH,
        )

    def forward_up(chunk, resid):
        size = resid.shape[0]
        base[chunk, :] = resid
        scale = lax.rsqrt(jnp.mean(resid * resid, axis=-1, keepdims=True) + EPS)
        scale_ref[chunk, :] = jnp.broadcast_to(scale, (size, 128))
        normed = (resid * scale).astype(BF16)
        normed_all[dp, chunk, :] = normed
        pre = dot_nn(normed, w1_t[...])
        pre_ref[chunk, :] = pre
        act[chunk, :] = (pre * jax.nn.sigmoid(pre)).astype(BF16)

    def forward_down(chunk):
        state[chunk, :] = (base[chunk, :] + dot_nn(act[chunk, :], w2[...])).astype(BF16)

    def backward(chunk, slope):
        back = dot_nn(slope.astype(BF16), w2_t[...])
        pre = pre_ref[chunk, :]
        sigma = jax.nn.sigmoid(pre)
        slope_h[chunk, :] = (back * (sigma * (1.0 + pre * (1.0 - sigma)))).astype(BF16)
        norm_slope = dot_nn(slope_h[chunk, :], w1[...])
        scale = scale_ref[chunk, 0:1]
        unit = base[chunk, :] * scale
        carry_all[dp, chunk, :] = (
            slope
            + scale * (norm_slope - unit * jnp.mean(norm_slope * unit, axis=-1, keepdims=True))
        ).astype(BF16)

    def rows_of(c, count):
        return pl.ds(pl.multiple_of(c * step_rows, step_rows), count * step_rows)

    every = pl.ds(0, rows)

    for i in range(3):
        for way in range(2):
            ring_copy(i, way, 0).start()
    for i in range(3):
        for way in range(2):
            pass_copy(i, way, 0).start()
        own_copy(i).start()

    for load in loads:
        load.wait()
    own_rows = pl.ds(pl.multiple_of(dp * rows, 128), rows)
    vocab = table_hbm.shape[0]
    picked = lax.broadcasted_iota(jnp.int32, (vocab, rows), 0) == token[:, own_rows]
    base[...] = dot_tn(picked.astype(F32).astype(BF16), w2_t[:vocab, :width])
    line = lax.broadcasted_iota(jnp.int32, (rows, rows), 0)
    column = lax.broadcasted_iota(jnp.int32, (rows, rows), 1)
    keep = jnp.where(line == column, mask[...].astype(F32), 0.0).astype(BF16)
    cot_ref[...] = dot_nn(keep, cot_ref[...]).astype(BF16)

    own_copy(0).wait()
    for way in range(2):
        add_base(dp, way)
    for step in range(1, chips):
        for i in range(3):
            for way in range(2):
                ring_copy(i, way, step - 1).wait_recv()
                if step < chips - 1:
                    ring_copy(i, way, step).start()
                pass_copy(i, way, step).start()
            if i == 0:
                for way in range(2):
                    add_base(origin_of(way, step), way)
                for way in range(2):
                    pass_copy(0, way, step - 1).wait_recv()
                    add_base(origin_of(way, step - 1) + 1 - 2 * core, way)
            if i == 1 and step == chips - 1:
                for way in range(2):
                    pass_copy(0, way, chips - 1).wait_recv()
                    add_base(origin_of(way, chips - 1) + 1 - 2 * core, way)
                own_copy(1).wait()
                for way in range(2):
                    for back in range(chips):
                        pass_copy(1, way, back).wait_recv()
                flip(w1, w1_t)

    quarter = term.shape[2]

    def quarter_of(q):
        return pl.ds(q * quarter, quarter)

    def up_copy(q, c):
        chunk = pl.ds(pl.multiple_of(c * step_rows, step_rows), step_rows)
        return pltpu.make_async_remote_copy(
            src_ref=term.at[q, chunk, :],
            dst_ref=term_in.at[q + 1, chunk, :],
            send_sem=up_send.at[q, c],
            recv_sem=up_recv.at[q, c],
            device_id=(dp, lax.rem(code + 1, n_code)),
            device_id_type=MESH,
        )

    def down_copy(q):
        return pltpu.make_async_remote_copy(
            src_ref=term.at[q],
            dst_ref=term_in.at[q],
            send_sem=down_send.at[q],
            recv_sem=down_recv.at[q],
            device_id=(dp, lax.rem(code + n_code - 1, n_code)),
            device_id_type=MESH,
        )

    def term_up(start, stop):
        def turn(c, carry):
            chunk = pl.ds(pl.multiple_of(c * step_rows, step_rows), step_rows)
            for q in reversed(range(1, n_code)):

                @pl.when(jnp.logical_and(jnp.logical_not(first), code <= q))
                def _():
                    up_copy(q, c).wait_recv()
                    term[q, chunk, :] = (
                        term[q, chunk, :].astype(F32) + term_in[q + 1, chunk, :].astype(F32)
                    ).astype(BF16)

                    @pl.when(code < q)
                    def _():
                        up_copy(q, c).start()

            return carry

        lax.fori_loop(start, stop, turn, 0)

    def term_down():
        for q in range(n_code - 1):

            @pl.when(jnp.logical_and(jnp.logical_not(last), code >= q))
            def _():
                down_copy(q).wait_recv()
                term[q] = (term[q].astype(F32) + term_in[q].astype(F32)).astype(BF16)

            @pl.when(code > q)
            def _():
                down_copy(q).start()

    @pl.when(first)
    def _():
        forward_up(every, base[...])

    own_copy(2).wait()
    for way in range(2):
        for step in range(chips):
            pass_copy(2, way, step).wait_recv()

    @pl.when(first)
    def _():
        forward_down(every)
        for c in range(CHUNKS):
            chain_copy(0, c).start()

    @pl.when(first)
    def _():
        for c in range(CHUNKS):
            spread(0, c)

    @pl.when(last)
    def _():
        slope_all[dp] = cot_ref[...]
        for c in range(CHUNKS):
            spread(1, c)

    for other in range(1, n_dp):
        swap_copy(0, other).start()
    cols_all[dp] = temporal[:, pl.ds(pl.multiple_of(dp * depth, 128), depth)]
    flip(w2, w2_t)

    def forward(c):
        chunk = rows_of(c, 1)
        chain_copy(0, c).wait_recv()
        forward_up(chunk, base[chunk, :] + incoming[chunk, :].astype(F32))
        spread(0, c)
        forward_down(chunk)

    @pl.when(jnp.logical_not(jnp.logical_or(first, last)))
    def _():
        def turn(c, carry):
            forward(c)
            chain_copy(0, c).start()
            return carry

        lax.fori_loop(0, CHUNKS, turn, 0)

    @pl.when(last)
    def _():
        def turn(h, carry):
            def inner(b, carry):
                forward(h * 2 + b)
                return carry

            lax.fori_loop(0, 2, inner, 0)
            pair = rows_of(h * 2, 2)
            backward(pair, cot_ref[pair, :].astype(F32))
            for b in range(2):
                chain_copy(1, h * 2 + b).start()
                spread(2, h * 2 + b)
            return carry

        lax.fori_loop(0, CHUNKS // 2, turn, 0)

    act_t[...] = act[...].T
    for other in range(1, n_dp):
        swap_copy(1, other).start()
    act_all[:, own_rows] = act_t[pl.ds(pl.multiple_of(dp * pad, 16), pad), :]

    @pl.when(first)
    def _():
        gather_forward(0)

    @pl.when(jnp.logical_not(last))
    def _():
        def turn(c, carry):
            chunk = rows_of(c, 1)
            chain_copy(1, c).wait_recv()
            slope = cot_ref[chunk, :].astype(F32) + returning[chunk, :].astype(F32)
            slope_all[dp, chunk, :] = slope.astype(BF16)
            spread(1, c)
            backward(chunk, slope)

            @pl.when(jnp.logical_not(first))
            def _():
                chain_copy(1, c).start()

            spread(2, c)

            @pl.when(first)
            def _():
                for q in reversed(range(n_code)):
                    term[q, chunk, :] = dot_nn(
                        carry_all[dp, chunk, :], proj_t[:, quarter_of(q)]
                    ).astype(BF16)
                    if q:
                        up_copy(q, c).start()

            return carry

        lax.fori_loop(0, CHUNKS, turn, 0)

    @pl.when(jnp.logical_not(first))
    def _():
        for q in range(n_code):
            term[q] = dot_nn(carry_all[dp], proj_t[:, quarter_of(q)]).astype(BF16)
            if q < n_code - 1:

                @pl.when(last)
                def _():
                    down_copy(q).start()

    pre_t[...] = slope_h[...].T
    for other in range(1, n_dp):
        swap_copy(2, other).start()
    pre_all[:, own_rows] = pre_t[pl.ds(pl.multiple_of(dp * pad, 16), pad), :]

    @pl.when(jnp.logical_not(first))
    def _():
        gather_forward(0)

    term_up(0, CHUNKS // 2)
    gather_forward(1)
    @pl.when(jnp.logical_not(last))
    def _():
        term_down()

    term_up(CHUNKS // 2, CHUNKS)
    gather_forward(2)

    def all_rows(array):
        return array[...].reshape(n_dp * rows, array.shape[2])

    def store(i):
        pairs = (
            (temporal_grad, temporal_out),
            (proj_grad, proj_out),
            (table_grad, table_out),
            (w1_grad, w1_out),
            (w2_grad, w2_out),
        )
        return pltpu.make_async_copy(pairs[i][0], pairs[i][1], store_sem.at[i])

    temporal_grad[...] = term[code]
    store(0).start()
    gather_finish(0)
    gather_finish(1)
    for other in range(1, n_dp):
        swap_copy(1, other).wait()
    w2_grad[...] = dot_nn(act_all[...], all_rows(slope_all)).astype(BF16)[:share]
    store(4).start()
    gather_finish(2)
    for other in range(1, n_dp):
        swap_copy(0, other).wait()
    carries = all_rows(carry_all)
    proj_grad[...] = dot_tn(all_rows(cols_all), carries).astype(BF16)
    store(1).start()
    piece = table_grad.shape[0]
    ids = lax.broadcasted_iota(jnp.int32, (piece, n_dp * rows), 0) + dp * piece
    table_grad[...] = dot_nn((ids == token[...]).astype(F32).astype(BF16), carries).astype(BF16)
    store(2).start()
    for other in range(1, n_dp):
        swap_copy(2, other).wait()
    w1_grad[...] = dot_nn(pre_all[...], all_rows(normed_all)).astype(BF16)[:share]
    store(3).start()

    for i in range(3):
        for way in range(2):
            for step in range(chips - 1):
                ring_copy(i, way, step).wait_send()
            for step in range(chips):
                pass_copy(i, way, step).wait_send()
    for c in range(CHUNKS):

        @pl.when(jnp.logical_not(last))
        def _():
            chain_copy(0, c).wait_send()

        @pl.when(jnp.logical_not(first))
        def _():
            chain_copy(1, c).wait_send()

    for q in range(n_code):

        @pl.when(code < q)
        def _():
            for c in range(CHUNKS):
                up_copy(q, c).wait_send()

        @pl.when(code > q)
        def _():
            down_copy(q).wait_send()

    for i in range(5):
        store(i).wait()


def copy_kernel(*refs):
    sources, targets, slots, (in_sem, out_sem) = refs[:5], refs[5:10], refs[10:15], refs[15:]
    takes = [pltpu.make_async_copy(sources[i], slots[i], in_sem.at[i]) for i in range(5)]
    gives = [pltpu.make_async_copy(slots[i], targets[i], out_sem.at[i]) for i in range(5)]
    for take in takes:
        take.start()
    for take, give in zip(takes, gives):
        take.wait()
        give.start()
    for give in gives:
        give.wait()


def per_device(
    temporal_out, depth_in, embed, depth_w1, depth_w2, audio_tokens, barge_mask, out_grad
):
    n_code = lax.axis_size("code")
    n_dp = lax.axis_size("dp")
    rows, wide = temporal_out.shape
    depth, width = depth_in.shape[1:]
    share = depth_w1.shape[2]
    pad = -(-share // 16) * 16
    hidden = pad * n_dp
    quarter = wide // n_code
    chips = n_dp // 2
    vocab = embed.shape[1]
    frames = audio_tokens.shape[0]
    extra = ((0, -share % 8), (0, 0))

    hbm = pl.BlockSpec(memory_space=pl.ANY)
    dma = pltpu.SemaphoreType.DMA
    out_shape = (
        jax.ShapeDtypeStruct((rows, quarter), BF16),
        jax.ShapeDtypeStruct((depth, width), BF16),
        jax.ShapeDtypeStruct((vocab // n_dp, width), BF16),
        jax.ShapeDtypeStruct((share, width), BF16),
        jax.ShapeDtypeStruct((share, width), BF16),
    )
    results = pl.pallas_call(
        functools.partial(chain_kernel, n_dp, n_code),
        out_shape=out_shape,
        in_specs=[hbm] * 8,
        out_specs=(hbm,) * 5,
        scratch_shapes=[
            pltpu.VMEM((rows, wide), BF16),
            pltpu.VMEM((rows, width), BF16),
            pltpu.VMEM((1, frames), jnp.int32),
            pltpu.VMEM((1, rows), jnp.int32),
            pltpu.VMEM((wide, width), BF16),
            pltpu.VMEM((hidden, width), BF16),
            pltpu.VMEM((hidden, width), BF16),
            pltpu.VMEM((width, wide), BF16),
            pltpu.VMEM((width, hidden), BF16),
            pltpu.VMEM((width, hidden), BF16),
            pltpu.VMEM((rows, width), F32),
            pltpu.VMEM((rows, width), BF16),
            pltpu.VMEM((rows, width), BF16),
            pltpu.VMEM((rows, width), BF16),
            pltpu.VMEM((rows, hidden), F32),
            pltpu.VMEM((rows, hidden), BF16),
            pltpu.VMEM((rows, hidden), BF16),
            pltpu.VMEM((hidden, rows), BF16),
            pltpu.VMEM((hidden, rows), BF16),
            pltpu.VMEM((rows, 128), F32),
            pltpu.VMEM((n_code, rows, quarter), BF16),
            pltpu.VMEM((n_code + 1, rows, quarter), BF16),
            pltpu.VMEM((n_dp, rows, depth), BF16),
            pltpu.VMEM((n_dp, rows, width), BF16),
            pltpu.VMEM((n_dp, rows, width), BF16),
            pltpu.VMEM((n_dp, rows, width), BF16),
            pltpu.VMEM((pad, frames), BF16),
            pltpu.VMEM((pad, frames), BF16),
            *(pltpu.VMEM(leaf.shape, BF16) for leaf in out_shape),
            dma((5,)),
            dma((3, 2, chips)),
            dma((3, 2, chips)),
            dma((3, 2, chips)),
            dma((3, 2, chips)),
            dma((3,)),
            dma((2, CHUNKS)),
            dma((2, CHUNKS)),
            dma((3, chips, CHUNKS)),
            dma((3, chips, CHUNKS)),
            dma((3, chips)),
            dma((3, chips)),
            dma((3, n_dp)),
            dma((3, n_dp)),
            dma((n_code, CHUNKS)),
            dma((n_code, CHUNKS)),
            dma((n_code,)),
            dma((n_code,)),
            dma((5,)),
        ],
        compiler_params=pltpu.CompilerParams(
            collective_id=0, has_side_effects=True, vmem_limit_bytes=63 * 1024 * 1024
        ),
        name="depth_chain",
    )(
        temporal_out,
        out_grad[:, 0, :],
        embed[0],
        audio_tokens.reshape(1, frames),
        barge_mask.reshape(1, rows),
        depth_in[0],
        jnp.pad(depth_w1[0].T, extra),
        jnp.pad(depth_w2[0].T, extra),
    )
    temporal_grad, proj_grad, table_grad, w1_grad, w2_grad = pl.pallas_call(
        copy_kernel,
        out_shape=out_shape,
        in_specs=[hbm] * 5,
        out_specs=(hbm,) * 5,
        scratch_shapes=[
            *(pltpu.VMEM(leaf.shape, BF16) for leaf in out_shape),
            dma((5,)),
            dma((5,)),
        ],
        name="results",
    )(*results)
    return (
        temporal_grad,
        proj_grad[None],
        table_grad[None],
        w1_grad.T[None],
        w2_grad.T[None],
    )


def solution(mesh):
    in_specs = (
        P("dp", None),
        P("code", "dp", None),
        P("code", None, None),
        P("code", None, "dp"),
        P("code", None, "dp"),
        P(None, "code"),
        P("dp"),
        P("dp", "code", None),
    )
    out_specs = (
        P("dp", "code"),
        P("code", "dp", None),
        P("code", "dp", None),
        P("code", None, "dp"),
        P("code", None, "dp"),
    )
    return jax.shard_map(
        per_device, mesh=mesh, in_specs=in_specs, out_specs=out_specs, check_vma=False
    )
```
